32 devices in a mesh: dp: 16 (over z, y, core), seq: 2 (over x).
Axes of the slice: x: 2, y: 2, z: 4, core: 2. Of those that a mesh axis runs over, the one named last changes fastest.
Arguments:
- queries: bfloat16 [4096, 1536], P(('dp', 'seq')), may hold values from -5 to 5
- keys: bfloat16 [4096, 1536], P(('dp', 'seq')), may hold values from -5 to 5
- values: bfloat16 [4096, 1536], P(('dp', 'seq')), may hold values from -6 to 6
- upstream: bfloat16 [4096, 1536], P(('dp', 'seq')), may hold values from -6 to 6
- out_weight: bfloat16 [1536, 1536], P('dp'), may hold values from -0.15625 to 0.15625
- clip_shape: int32 [16, 2, 3], P('dp'), may hold values from 1 to 3, as said below
- slot_tile: int32 [16, 8], P('dp'), may hold values from 0 to 7, each once within a row
Outputs:
- mixed_out: bfloat16 [4096, 1536], P(('dp', 'seq'))
- query_grad: bfloat16 [4096, 1536], P(('dp', 'seq'))
- key_grad: bfloat16 [4096, 1536], P(('dp', 'seq'))
- value_grad: bfloat16 [4096, 1536], P(('dp', 'seq'))
- weight_grad: float32 [1536, 1536], P('dp')
The draws below stay inside these ranges and needn't reach their ends.
Inputs may be any that keep to these rules, and one draw needn't show every extreme that they name: `clip_shape`: in every batch the clips' tile counts add up to 8; a clip is 1 or 2 tiles long in time and 2 tiles high.
All inputs are finite; a program needn't handle non-finite values.
Results may differ from the reference program's by a relative error of at most 0.02.
Values may be sent and summed in bfloat16 or wider, within the bound.
No kernel may reach another device: no remote copies, remote signals or barrier semaphores. Data moves between devices by JAX's collectives and lax.ppermute only.
A program may use at most 128 MiB of HBM per device.

```python
import jax
import jax.numpy as jnp
from jax import lax

HEADS = 12
HEAD_DIM = 128
DO = 1536
TILE = 32
HD = 1536
G = 8
TOKENS = 4096
N_DP = 16


def shared_pair(key):
    base = jax.random.fold_in(key, 11)
    streams = jax.random.split(base, 2)
    query_draw = jnp.clip(jax.random.normal(streams[0], (TOKENS, HD), jnp.float32), -5.0, 5.0)
    key_draw = jnp.clip(jax.random.normal(streams[1], (TOKENS, HD), jnp.float32), -5.0, 5.0)
    return (query_draw, key_draw)


def draw_queries(key, part):
    return shared_pair(key)[0].astype(jnp.bfloat16)


def draw_keys(key, part):
    return shared_pair(key)[1].astype(jnp.bfloat16)


def draw_clip_shape(key, part):
    half_slots = G // 2
    batch_index = jnp.arange(N_DP, dtype=jnp.int32)
    first_area = jax.random.randint(jax.random.fold_in(key, 5), (N_DP,), 1, half_slots).astype(jnp.int32)
    first_area = jnp.where(batch_index == 0, 1, first_area).astype(jnp.int32)
    first_coin = jax.random.randint(jax.random.fold_in(key, 6), (N_DP,), 0, 2).astype(jnp.int32)
    first_time = jnp.where((first_area % 2 == 0) & (first_coin == 1), 2, 1).astype(jnp.int32)
    first_wide = (first_area // first_time).astype(jnp.int32)
    second_area = (half_slots - first_area).astype(jnp.int32)
    second_coin = jax.random.randint(jax.random.fold_in(key, 7), (N_DP,), 0, 2).astype(jnp.int32)
    second_time = jnp.where((second_area % 2 == 0) & (second_coin == 1) & (batch_index != 0), 2, 1).astype(jnp.int32)
    second_wide = (second_area // second_time).astype(jnp.int32)
    unit_row = jnp.ones((N_DP,), jnp.int32)
    first_clip = jnp.stack([first_time, 2 * unit_row, first_wide], axis=1)
    second_clip = jnp.stack([second_time, 2 * unit_row, second_wide], axis=1)
    return jnp.stack([first_clip, second_clip], axis=1).astype(jnp.int32)


def spiked(result, key, source, target, blocks, factor):
    def block_of(axis_at):
        return (jnp.arange(result.shape[axis_at]) // (result.shape[axis_at] // blocks)).reshape((-1,) + (1,) * (result.ndim - 1 - axis_at))

    first = jax.random.permutation(key, blocks)[block_of(target)]
    far = (block_of(target) + blocks // 2) % blocks
    return jnp.where((block_of(source) == first) | (block_of(source) == far), factor * result, result)


def steps_of(rng, extent, shards, least, top_value):
    loudness = 1.0
    for dim, parts in shards:
        steps = jax.random.uniform(jax.random.fold_in(jax.random.fold_in(rng, 6), dim), (parts,), jnp.float32, least / len(shards), top_value / len(shards))
        loudness = loudness * jnp.repeat(jnp.exp(steps), extent[dim] // parts).reshape((-1,) + (1,) * (len(extent) - 1 - dim))
    return loudness


def noise(rng, extent, scale, reach, cuts=(), kind=jnp.bfloat16):
    array = jax.random.normal(rng, extent, jnp.float32) * scale
    if len(cuts) > 0:
        array = steps_of(rng, extent, cuts, -0.22, 0.18) * array
    return jnp.clip(array, min=-reach, max=reach).astype(kind)


def bell_draw_with(rng, extent, scale, bound, cuts, heavy, kind=jnp.bfloat16):
    entries = scale * jax.random.normal(rng, extent, jnp.float32)
    if cuts:
        entries = entries * steps_of(rng, extent, cuts, -0.22, 0.18)
    return jnp.clip(spiked(entries, jax.random.fold_in(rng, 3), *heavy), -bound, bound).astype(kind)


def setup_inputs(seed: int = 0) -> dict:
    streams_of = jax.random.split(jax.random.key(seed), 8)
    return {
        "queries": draw_queries(jax.random.fold_in(streams_of[7], 71), 0),
        "keys": draw_keys(jax.random.fold_in(streams_of[7], 71), 0),
        "values": noise(streams_of[2], (TOKENS, HD), 1.0, 6.0, ((0, 32),)),
        "upstream": bell_draw_with(streams_of[3], (TOKENS, DO), 1.0, 6.0, ((0, 32),), (0, 1, 32, 2.75)),
        "out_weight": noise(streams_of[4], (DO, HD), HD ** -0.5, 0.15625, ((0, 16),)),
        "clip_shape": draw_clip_shape(jax.random.fold_in(streams_of[7], 71), 0),
        "slot_tile": jax.vmap(lambda own: jax.random.permutation(own, G))(jax.random.split(streams_of[6], N_DP)).reshape((N_DP, G)).astype(jnp.int32),
    }


def tile_place(clip_dims, tile_ids):
    clip_sizes = (clip_dims[:, 0] * clip_dims[:, 1] * clip_dims[:, 2]).astype(jnp.int32)
    clip_starts = (jnp.cumsum(clip_sizes) - clip_sizes).astype(jnp.int32)
    clip_of = (jnp.sum((tile_ids[:, None] >= clip_starts[None, :]).astype(jnp.int32), axis=1) - 1).astype(jnp.int32)
    chooser = (clip_of[:, None] == jnp.arange(clip_dims.shape[0], dtype=jnp.int32)[None, :]).astype(jnp.int32)
    first_tile = jnp.sum(chooser * clip_starts[None, :], axis=1).astype(jnp.int32)
    high_tiles = jnp.sum(chooser * clip_dims[None, :, 1], axis=1).astype(jnp.int32)
    wide_tiles = jnp.sum(chooser * clip_dims[None, :, 2], axis=1).astype(jnp.int32)
    offset = tile_ids - first_tile
    return (clip_of, offset // (wide_tiles * high_tiles), (offset // wide_tiles) % high_tiles, offset % wide_tiles)


def tile_window(place_rows, place_cols):
    inside = place_rows[0][:, None] == place_cols[0][None, :]
    for dimension in range(1, 4):
        inside = inside & (jnp.abs(place_rows[dimension][:, None] - place_cols[dimension][None, :]) <= 1)
    return inside


def attend_group(queries, keys, values, upstream, out_weight, clip_dims, slot_list):
    group_rows = queries.shape[0]
    scaling = HEAD_DIM ** -0.5
    token_tiles = slot_list[jnp.arange(group_rows, dtype=jnp.int32) // TILE]
    placing = tile_place(clip_dims, token_tiles)
    allowed = tile_window(placing, placing)
    query3 = queries.astype(jnp.float32).reshape(group_rows, HEADS, HEAD_DIM)
    key3 = keys.astype(jnp.float32).reshape(group_rows, HEADS, HEAD_DIM)
    value3 = values.astype(jnp.float32).reshape(group_rows, HEADS, HEAD_DIM)
    scores = jnp.einsum("ihd,jhd->hij", query3, key3) * scaling
    scores = jnp.where(allowed[None], scores, -jnp.inf)
    row_max = jnp.max(scores, axis=2)
    exponent = jnp.exp(scores - row_max[:, :, None])
    row_sum = jnp.sum(exponent, axis=2)
    weights = lax.optimization_barrier(exponent.astype(jnp.bfloat16))
    mixed = jnp.einsum("hij,jhd->ihd", weights.astype(jnp.float32), value3) / jnp.transpose(row_sum)[:, :, None]
    attended = lax.optimization_barrier(mixed.reshape(group_rows, HEADS * HEAD_DIM).astype(jnp.bfloat16))
    mixed_out = jnp.dot(attended, out_weight.T, preferred_element_type=jnp.float32).astype(jnp.bfloat16)
    grad_out = lax.optimization_barrier(jnp.dot(upstream, out_weight, preferred_element_type=jnp.float32).astype(jnp.bfloat16))
    grad3 = grad_out.astype(jnp.float32).reshape(group_rows, HEADS, HEAD_DIM)
    attended3 = attended.astype(jnp.float32).reshape(group_rows, HEADS, HEAD_DIM)
    inner_sum = jnp.transpose(jnp.sum(grad3 * attended3, axis=2))
    log_total = row_max + jnp.log(row_sum)
    prob_full = jnp.exp(scores - log_total[:, :, None])
    slope = jnp.einsum("ihd,jhd->hij", grad3, value3)
    score_grad = lax.optimization_barrier((prob_full * (slope - inner_sum[:, :, None])).astype(jnp.bfloat16)).astype(jnp.float32)
    prob_low = lax.optimization_barrier(prob_full.astype(jnp.bfloat16)).astype(jnp.float32)
    query_grad = (jnp.einsum("hij,jhd->ihd", score_grad, key3) * scaling).reshape(group_rows, -1).astype(jnp.bfloat16)
    key_grad = (jnp.einsum("hij,ihd->jhd", score_grad, query3) * scaling).reshape(group_rows, -1).astype(jnp.bfloat16)
    value_grad = jnp.einsum("hij,ihd->jhd", prob_low, grad3).reshape(group_rows, -1).astype(jnp.bfloat16)
    weight_part = jnp.dot(upstream.T, attended, preferred_element_type=jnp.float32)
    return mixed_out, query_grad, key_grad, value_grad, weight_part


def reference(queries, keys, values, upstream, out_weight, clip_shape, slot_tile):
    group_rows = queries.shape[0] // N_DP

    def one_group(group_items):
        return attend_group(group_items[0], group_items[1], group_items[2], group_items[3], out_weight, group_items[4], group_items[5])

    stacked = (queries.reshape(N_DP, group_rows, -1), keys.reshape(N_DP, group_rows, -1), values.reshape(N_DP, group_rows, -1), upstream.reshape(N_DP, group_rows, -1), clip_shape, slot_tile)
    results = lax.map(one_group, stacked)
    mixed_out = results[0].reshape(queries.shape[0], -1)
    query_grad = results[1].reshape(queries.shape[0], -1)
    key_grad = results[2].reshape(queries.shape[0], -1)
    value_grad = results[3].reshape(queries.shape[0], -1)
    weight_grad = jnp.sum(results[4], axis=0)
    return (mixed_out, query_grad, key_grad, value_grad, weight_grad)
```

```python
import functools

import jax
import jax.numpy as jnp
from jax import lax
from jax.experimental import pallas as pl
from jax.experimental.pallas import tpu as pltpu
from jax.sharding import PartitionSpec as P

HEADS = 12
HEAD_DIM = 128
TILE = 32
F32 = jnp.float32
BF16 = jnp.bfloat16


def tile_place(clip_dims, tile_ids):
    clip_sizes = clip_dims[:, 0] * clip_dims[:, 1] * clip_dims[:, 2]
    clip_starts = jnp.cumsum(clip_sizes) - clip_sizes
    clip_of = jnp.sum((tile_ids[:, None] >= clip_starts[None, :]).astype(jnp.int32), axis=1) - 1
    chooser = (clip_of[:, None] == jnp.arange(clip_dims.shape[0], dtype=jnp.int32)[None, :]).astype(
        jnp.int32
    )
    first_tile = jnp.sum(chooser * clip_starts[None, :], axis=1)
    high_tiles = jnp.sum(chooser * clip_dims[None, :, 1], axis=1)
    wide_tiles = jnp.sum(chooser * clip_dims[None, :, 2], axis=1)
    offset = tile_ids - first_tile
    return (
        clip_of,
        offset // (wide_tiles * high_tiles),
        offset // wide_tiles % high_tiles,
        offset % wide_tiles,
    )


def tile_window(place_rows, place_cols):
    inside = place_rows[0][:, None] == place_cols[0][None, :]
    for dimension in range(1, 4):
        inside = inside & (
            jnp.abs(place_rows[dimension][:, None] - place_cols[dimension][None, :]) <= 1
        )
    return inside


def per_device(queries, keys, values, upstream, out_weight, clip_shape, slot_tile):
    row_count = queries.shape[0]
    feat_count = queries.shape[1]
    scaling = HEAD_DIM ** (-0.5)
    clip_dims = clip_shape[0]
    slot_list = slot_tile[0]
    local_tiles = row_count // TILE
    own_seat = lax.axis_index("seq")
    own_slots = lax.dynamic_slice_in_dim(slot_list, own_seat * local_tiles, local_tiles)
    own_tokens = own_slots[jnp.arange(row_count, dtype=jnp.int32) // TILE]
    all_tokens = slot_list[jnp.arange(slot_list.shape[0] * TILE, dtype=jnp.int32) // TILE]
    own_place = tile_place(clip_dims, own_tokens)
    all_place = tile_place(clip_dims, all_tokens)
    allowed = tile_window(own_place, all_place)
    full_weight = lax.all_gather(out_weight, "dp", axis=0, tiled=True)
    key_all, value_all = (
        lax.all_gather(keys, "seq", axis=0, tiled=True),
        lax.all_gather(values, "seq", axis=0, tiled=True),
    )
    group_tokens = key_all.shape[0]
    query3 = queries.reshape(row_count, HEADS, HEAD_DIM)
    key_all3 = key_all.reshape(group_tokens, HEADS, HEAD_DIM)
    value_all3 = value_all.reshape(group_tokens, HEADS, HEAD_DIM)
    scores = (
        jnp.einsum("ihd,jhd->hij", query3, key_all3, preferred_element_type=jnp.float32) * scaling
    )
    scores = jnp.where(allowed[None], scores, -jnp.inf)
    row_max = jnp.max(scores, axis=2)
    exponent = jnp.exp(scores - row_max[:, :, None])
    row_sum = jnp.sum(exponent, axis=2)
    weights = exponent.astype(jnp.bfloat16)
    mixed = (
        jnp.einsum("hij,jhd->ihd", weights, value_all3, preferred_element_type=jnp.float32)
        / jnp.transpose(row_sum)[:, :, None]
    )
    attended = mixed.reshape(row_count, feat_count).astype(jnp.bfloat16)
    mixed_out = jnp.einsum(
        "id,od->io", attended, full_weight, preferred_element_type=jnp.float32
    ).astype(jnp.bfloat16)
    grad_out = jnp.dot(upstream, full_weight, preferred_element_type=jnp.float32).astype(
        jnp.bfloat16
    )
    grad3 = grad_out.reshape(row_count, HEADS, HEAD_DIM)
    attended3 = attended.reshape(row_count, HEADS, HEAD_DIM)
    inner_sum = jnp.transpose(
        jnp.sum(grad3.astype(jnp.float32) * attended3.astype(jnp.float32), axis=2)
    )
    log_total = row_max + jnp.log(row_sum)
    prob_full = jnp.exp(scores - log_total[:, :, None])
    slope = jnp.einsum("ihd,jhd->hij", grad3, value_all3, preferred_element_type=jnp.float32)
    score_grad = (prob_full * (slope - inner_sum[:, :, None])).astype(jnp.bfloat16)
    query_grad = (
        (
            jnp.einsum("hij,jhd->ihd", score_grad, key_all3, preferred_element_type=jnp.float32)
            * scaling
        )
        .reshape(row_count, feat_count)
        .astype(jnp.bfloat16)
    )
    prob_low = prob_full.astype(jnp.bfloat16)
    key_part = (
        jnp.einsum("hij,ihd->jhd", score_grad, query3, preferred_element_type=jnp.float32) * scaling
    )
    value_part = jnp.einsum("hij,ihd->jhd", prob_low, grad3, preferred_element_type=jnp.float32)
    key_value_grad = lax.psum_scatter(
        jnp.concatenate(
            [
                key_part.reshape(row_count * lax.axis_size("seq"), feat_count),
                value_part.reshape(row_count * lax.axis_size("seq"), feat_count),
            ],
            axis=1,
        ),
        "seq",
        scatter_dimension=0,
        tiled=True,
    )
    key_grad = key_value_grad[:, :feat_count].astype(jnp.bfloat16)
    value_grad = key_value_grad[:, feat_count:].astype(jnp.bfloat16)
    grad_piece = lax.psum_scatter(
        jnp.einsum("io,id->od", upstream, attended, preferred_element_type=jnp.float32),
        "dp",
        scatter_dimension=0,
        tiled=True,
    )
    weight_grad = lax.psum(grad_piece, "seq")
    return (mixed_out, query_grad, key_grad, value_grad, weight_grad)


def swap(block, axis, bit):
    size = lax.axis_size(axis)
    return lax.ppermute(block, axis, [(i, i ^ bit) for i in range(size)])


def dot_nt(left, right):
    return lax.dot_general(left, right, (((1,), (1,)), ((), ())), preferred_element_type=F32)


def dot_tn(left, right):
    return lax.dot_general(left, right, (((0,), (0,)), ((), ())), preferred_element_type=F32)


def dot_nn(left, right):
    return lax.dot_general(left, right, (((1,), (0,)), ((), ())), preferred_element_type=F32)


def place_of(clip_ref, tile):
    clip_count = clip_ref.shape[1]
    start = jnp.int32(0)
    clip_at, first, high, wide = jnp.int32(-1), jnp.int32(0), jnp.int32(1), jnp.int32(1)
    for c in range(clip_count):
        inside = tile >= start
        clip_at = jnp.where(inside, c, clip_at)
        first = jnp.where(inside, start, first)
        high = jnp.where(inside, clip_ref[0, c, 1], high)
        wide = jnp.where(inside, clip_ref[0, c, 2], wide)
        start = start + clip_ref[0, c, 0] * clip_ref[0, c, 1] * clip_ref[0, c, 2]
    offset = tile - first
    line = lax.div(offset, wide)
    return clip_at, lax.div(line, high), lax.rem(line, high), lax.rem(offset, wide)


def attend_kernel(seat_ref, clip_ref, slot_ref, q_own, k_own, v_own, q_far, k_far, v_far,
                  attended_ref, prob_ref, bias_ref):
    rows = q_own.shape[0]
    tokens = 2 * rows
    tiles = tokens // TILE
    seat = seat_ref[0]
    places = []
    for t in range(tiles):
        slot = lax.rem(seat * (tiles // 2) + t, tiles)
        places.append(place_of(clip_ref, slot_ref[0, slot]))
    lane_tile = lax.broadcasted_iota(jnp.int32, (TILE, tokens), 1) // TILE
    lane_places = []
    for d in range(4):
        lane = jnp.full((TILE, tokens), places[0][d], jnp.int32)
        for t in range(1, tiles):
            lane = jnp.where(lane_tile == t, places[t][d], lane)
        lane_places.append(lane)
    for t in range(tiles):
        inside = lane_places[0] == places[t][0]
        for d in range(1, 4):
            inside = inside & (jnp.abs(lane_places[d] - places[t][d]) <= 1)
        bias_ref[pl.ds(t * TILE, TILE), :] = jnp.where(inside, 0.0, -jnp.inf)
    scaling = HEAD_DIM ** (-0.5)
    for h in range(q_own.shape[1] // HEAD_DIM):
        cols = slice(h * HEAD_DIM, (h + 1) * HEAD_DIM)
        q = jnp.concatenate([q_own[:, cols], q_far[:, cols]], axis=0)
        k = jnp.concatenate([k_own[:, cols], k_far[:, cols]], axis=0)
        v = jnp.concatenate([v_own[:, cols], v_far[:, cols]], axis=0)
        scores = dot_nt(q, k) * scaling + bias_ref[...]
        exponent = jnp.exp(scores - jnp.max(scores, axis=1, keepdims=True))
        row_sum = jnp.sum(exponent, axis=1, keepdims=True)
        prob_ref[h] = exponent / row_sum
        attended_ref[:, cols] = (dot_nn(exponent.astype(BF16), v) / row_sum).astype(BF16)


def turn_kernel(dp_ref, up_own, up_far, keep_ref, send_ref, turned_ref, *, order, width):
    rows = up_own.shape[0]
    turned_ref[:, :rows] = up_own[...].T
    turned_ref[:, rows:] = up_far[...].T
    for r, bits in enumerate(order):
        mine = pl.multiple_of((dp_ref[0] ^ bits) * width, width)
        theirs = pl.multiple_of((dp_ref[0] ^ bits ^ 1) * width, width)
        keep_ref[pl.ds(r * width, width), :] = turned_ref[pl.ds(mine, width), :]
        send_ref[pl.ds(r * width, width), :] = turned_ref[pl.ds(theirs, width), :]


def mix_kernel(dp_ref, attended_ref, *refs):
    pieces, (weight_ref, own_ref, send_ref) = refs[:-3], refs[-3:]
    width = pieces[0].shape[0]
    for bits, piece in enumerate(pieces):
        at = pl.multiple_of((dp_ref[0] ^ bits) * width, width)
        weight_ref[pl.ds(at, width), :] = piece[...]
    rows = own_ref.shape[0]
    weight = weight_ref[...]
    send_ref[...] = dot_nt(attended_ref[rows:, :], weight).astype(BF16)
    own_ref[...] = dot_nt(attended_ref[:rows, :], weight)


def outer_kernel(keep_up, far_up, own_at, far_at, send_ref, keep_ref):
    half = send_ref.shape[0]
    total = dot_nn(keep_up[...], own_at[...]) + dot_nn(far_up[...], far_at[...])
    send_ref[...] = total[:half].astype(BF16)
    keep_ref[...] = total[half:]


def back_kernel(seat_ref, up_own, up_far, weight_ref, attended_ref, prob_ref,
                q_own, k_own, v_own, q_far, k_far, v_far,
                dq_own, dk_own, dv_own, dq_far, dk_far, dv_far, grad_ref):
    rows = q_own.shape[0]
    scaling = HEAD_DIM ** (-0.5)
    weight = weight_ref[...]
    grad_ref[:rows, :] = dot_nn(up_own[...], weight).astype(BF16)
    grad_ref[rows:, :] = dot_nn(up_far[...], weight).astype(BF16)
    for h in range(q_own.shape[1] // HEAD_DIM):
        cols = slice(h * HEAD_DIM, (h + 1) * HEAD_DIM)
        q = jnp.concatenate([q_own[:, cols], q_far[:, cols]], axis=0)
        k = jnp.concatenate([k_own[:, cols], k_far[:, cols]], axis=0)
        v = jnp.concatenate([v_own[:, cols], v_far[:, cols]], axis=0)
        grad = grad_ref[:, cols]
        inner = jnp.sum(grad.astype(F32) * attended_ref[:, cols].astype(F32), axis=1, keepdims=True)
        prob = prob_ref[h]
        score_grad = (prob * (dot_nt(grad, v) - inner)).astype(BF16)
        dq = (dot_nn(score_grad, k) * scaling).astype(BF16)
        dk = (dot_tn(score_grad, q) * scaling).astype(BF16)
        dv = dot_tn(prob.astype(BF16), grad).astype(BF16)
        for value, own, far in ((dq, dq_own, dq_far), (dk, dk_own, dk_far), (dv, dv_own, dv_far)):
            own[:, cols] = value[:rows]
            far[:, cols] = value[rows:]


def whole(shape):
    return pl.BlockSpec(shape, lambda i, *refs: (0,) * len(shape))


def call(kernel, scalars, inputs, in_specs, outs, scratch=()):
    specs = [whole(a.shape) if s is None else s for a, s in zip(inputs, in_specs)]
    return pl.pallas_call(
        kernel,
        grid_spec=pltpu.PrefetchScalarGridSpec(
            num_scalar_prefetch=len(scalars),
            grid=(1,),
            in_specs=specs,
            out_specs=[whole(o.shape) for o in outs],
            scratch_shapes=list(scratch),
        ),
        out_shape=outs,
    )(*scalars, *inputs)


def split_heads(queries, keys, values, upstream, out_weight, clip_shape, slot_tile):
    rows, feats = queries.shape
    half = feats // 2
    heads = half // HEAD_DIM
    width = out_weight.shape[0]
    out_feats = upstream.shape[1]
    dp_size = lax.axis_size("dp")
    seat = lax.axis_index("seq").astype(jnp.int32)
    spot = lax.axis_index("dp").astype(jnp.int32)
    seat1, spot1 = seat.reshape(1), spot.reshape(1)
    like = jax.ShapeDtypeStruct

    def half_of(array, which):
        return lax.dynamic_slice_in_dim(array, which * half, half, axis=1)

    q_far = swap(half_of(queries, 1 - seat), "seq", 1)
    k_far = swap(half_of(keys, 1 - seat), "seq", 1)
    v_far = swap(half_of(values, 1 - seat), "seq", 1)
    up_far = swap(upstream, "seq", 1)

    pieces = {0: half_of(out_weight, seat)}
    line_bits = list(range(0, dp_size, 4))
    top = 4
    while top < dp_size:
        pieces[top] = swap(pieces[0], "dp", top)
        for low in range(4, top, 4):
            pieces[top | low] = swap(pieces[top], "dp", low)
        top *= 2
    for bits in line_bits:
        pieces[bits | 2] = swap(pieces[bits], "dp", 2)
    for bits in range(0, dp_size, 2):
        pieces[bits | 1] = swap(pieces[bits], "dp", 1)

    own_half = pl.BlockSpec((rows, half), lambda i, seat_ref, *refs: (0, seat_ref[0]))
    attended, prob = call(
        attend_kernel, (seat1, clip_shape, slot_tile),
        (queries, keys, values, q_far, k_far, v_far), (own_half,) * 3 + (None,) * 3,
        [like((2 * rows, half), BF16), like((heads, 2 * rows, 2 * rows), F32)],
        [pltpu.VMEM((2 * rows, 2 * rows), F32)],
    )
    order = [bits | 2 for bits in line_bits] + line_bits
    up_rows = len(order) * width
    keep_up, send_up = call(
        functools.partial(turn_kernel, order=order, width=width), (spot1,),
        (upstream, up_far), (None, None),
        [like((up_rows, 2 * rows), BF16)] * 2,
        [pltpu.VMEM((out_feats, 2 * rows), BF16)],
    )
    far_up = swap(send_up, "dp", 1)
    far_at = swap(attended, "dp", 1)
    weight, mixed_own, mixed_send = call(
        mix_kernel, (spot1,),
        (attended, *[pieces[bits] for bits in range(dp_size)]), (None,) * (dp_size + 1),
        [like((out_feats, half), BF16), like((rows, out_feats), F32), like((rows, out_feats), BF16)],
    )
    mixed_far = swap(mixed_send, "seq", 1)
    outer_send, outer_keep = call(
        outer_kernel, (), (keep_up, far_up, attended, far_at), (None,) * 4,
        [like((up_rows // 2, half), BF16), like((up_rows // 2, half), F32)],
    )
    outer_far = swap(outer_send, "dp", 2)
    grads = call(
        back_kernel, (seat1,),
        (upstream, up_far, weight, attended, prob, queries, keys, values, q_far, k_far, v_far),
        (None,) * 5 + (own_half,) * 3 + (None,) * 3,
        [like((rows, half), BF16)] * 6,
        [pltpu.VMEM((2 * rows, half), BF16)],
    )

    def joined(own, far):
        return jnp.where(seat == 0, jnp.concatenate([own, far], axis=1), jnp.concatenate([far, own], axis=1))

    dqkv = [joined(grads[n], swap(grads[n + 3], "seq", 1)) for n in range(3)]
    mixed_out = (mixed_own + mixed_far.astype(F32)).astype(BF16)
    line = outer_keep + outer_far.astype(F32)
    total = line[:width]
    for n in range(1, len(line_bits)):
        block = line[n * width:(n + 1) * width].astype(BF16)
        total = total + swap(block, "dp", line_bits[n]).astype(F32)
    other = swap(total.astype(BF16), "seq", 1).astype(F32)
    weight_grad = joined(total, other)
    return (mixed_out, *dqkv, weight_grad)


def splits(mesh):
    dp_size, seats = mesh.shape["dp"], mesh.shape["seq"]
    return seats == 2 and HEADS % 2 == 0 and dp_size >= 4 and dp_size & (dp_size - 1) == 0


def solution(mesh):
    return jax.shard_map(
        split_heads if splits(mesh) else per_device,
        mesh=mesh,
        in_specs=(
            P(("dp", "seq"), None),
            P(("dp", "seq"), None),
            P(("dp", "seq"), None),
            P(("dp", "seq"), None),
            P("dp", None),
            P("dp", None, None),
            P("dp", None),
        ),
        out_specs=(
            P(("dp", "seq"), None),
            P(("dp", "seq"), None),
            P(("dp", "seq"), None),
            P(("dp", "seq"), None),
            P("dp", None),
        ),
        check_vma=False,
    )
```
